32 devices in a mesh: rows: 4 (over x, core), slopes: 8 (over z, y).
Axes of the slice: x: 2, y: 2, z: 4, core: 2. Of those that a mesh axis runs over, the one named last changes fastest.
Arguments:
- reconstructor: bfloat16 [5120, 90112], P('rows', 'slopes'), may hold values from -0.375 to 0.375
- cov_slab: bfloat16 [90112, 256], P('slopes', 'rows'), may hold values from -0.4375 to 0.4375
- residual_in: float32 [5120, 5120], P('rows', 'slopes'), may hold values from -6 to 6
- propagation: bfloat16 [5120, 5120], P('rows', 'slopes'), may hold values from -0.078125 to 0.078125
Outputs:
- residual_out: float32 [5120, 5120], P('rows', 'slopes')
- projected: float32 [5120, 5120], P('rows', 'slopes')
The draws below stay inside these ranges and needn't reach their ends.
All inputs are finite; a program needn't handle non-finite values.
Results may differ from the reference program's by a relative error of at most 0.0046.
Values may be sent and summed in bfloat16 or wider, within the bound.
No kernel may reach another device: no remote copies, remote signals or barrier semaphores. Data moves between devices by JAX's collectives and lax.ppermute only.
A program may use at most 128 MiB of HBM per device.

```python
import jax
import jax.numpy as jnp
from jax import lax

A = 5120
SLOPES = 90112
SLAB = 256
STRIDE = 352


def strengthened(result, own_key, source, target, shards_of, factor):
    def block_of(dim):
        return (jnp.arange(result.shape[dim]) // (result.shape[dim] // shards_of)).reshape((-1,) + (1,) * (result.ndim - 1 - dim))

    one_side = jax.random.permutation(own_key, shards_of)[block_of(target)]
    second = (block_of(target) + shards_of // 2) % shards_of
    return jnp.where((block_of(source) == one_side) | (block_of(source) == second), factor * result, result)


def shard_levels(rng, shape, cuts, smallest, high):
    factor_of = 1.0
    for axis_at, shards_of in cuts:
        draws = jax.random.uniform(jax.random.fold_in(jax.random.fold_in(rng, 6), axis_at), (shards_of,), jnp.float32, smallest / len(cuts), high / len(cuts))
        factor_of = factor_of * jnp.repeat(jnp.exp(draws), shape[axis_at] // shards_of).reshape((-1,) + (1,) * (len(shape) - 1 - axis_at))
    return factor_of


def normal_values(key, shape, width, most, split=(), kind=jnp.bfloat16):
    entries = jax.random.normal(key, shape, jnp.float32) * width
    if len(split) > 0:
        entries = shard_levels(key, shape, split, -0.22, 0.18) * entries
    return jnp.clip(entries, min=-most, max=most).astype(kind)


def heavy_noise(key, extent, spread, limit, split, heavy, dtype=jnp.bfloat16):
    entries = spread * jax.random.normal(key, extent, jnp.float32)
    if split:
        entries = entries * shard_levels(key, extent, split, -0.22, 0.18)
    return jnp.clip(strengthened(entries, jax.random.fold_in(key, 3), *heavy), -limit, limit).astype(dtype)


def setup_inputs(seed: int = 0) -> dict:
    key_of = jax.random.split(jax.random.key(seed), 5)
    return {
        "reconstructor": normal_values(key_of[0], (A, SLOPES), SLAB ** -0.5, 0.375, ((0, 4), (1, 8))),
        "cov_slab": heavy_noise(key_of[1], (SLOPES, SLAB), STRIDE ** -0.5, 0.4375, ((0, 8), (1, 4)), (0, 1, 8, 2.0)),
        "residual_in": normal_values(key_of[2], (A, A), 1.0, 6.0, ((0, 4), (1, 8)), jnp.float32),
        "propagation": normal_values(key_of[3], (A, A), A ** -0.5, 0.078125, ((0, 4), (1, 8))),
    }


def reference(reconstructor, cov_slab, residual_in, propagation):
    block = 512 if A % 512 == 0 else A
    cov_wide = cov_slab.astype(jnp.float32)

    def one_block(recon_rows):
        return jnp.dot(recon_rows.astype(jnp.float32), cov_wide, preferred_element_type=jnp.float32)

    blocks = reconstructor.reshape(A // block, block, SLOPES)
    reach = lax.map(one_block, blocks).reshape(A, SLAB).astype(jnp.bfloat16)
    picked = reconstructor[:, ::STRIDE]
    residual_out = residual_in + jnp.dot(reach, picked.T, preferred_element_type=jnp.float32)
    resid_low = residual_out.astype(jnp.bfloat16)
    front = jnp.dot(propagation, resid_low, preferred_element_type=jnp.float32).astype(jnp.bfloat16)
    projected = jnp.dot(front, propagation.T, preferred_element_type=jnp.float32)
    return residual_out, projected
```

```python
import jax
import jax.numpy as jnp
from jax import lax
from jax.sharding import PartitionSpec as P

BF = jnp.bfloat16
F32 = jnp.float32
CORES = 2


def dot(a, b, ca, cb):
    return lax.dot_general(a, b, (((ca,), (cb,)), ((), ())), preferred_element_type=F32)


def make_body(rows, slopes):
    nx = rows // CORES
    nz = rows
    ny = slopes // rows

    def body(reconstructor, cov_slab, residual_in, propagation):
        r = lax.axis_index("rows")
        s = lax.axis_index("slopes")
        x, z, y = r // CORES, s // ny, s % ny
        m, w = propagation.shape
        h = m // ny
        slab = cov_slab.shape[1] * rows
        stride = reconstructor.shape[1] * slopes // slab

        def to_y(a):
            return lax.ppermute(a, "slopes", [(i, i ^ 1) for i in range(slopes)])

        def to_core(a):
            return lax.ppermute(a, "rows", [(i, i ^ 1) for i in range(rows)])

        def to_x(a, k):
            return lax.ppermute(a, "rows", [(i, (i + CORES * k) % rows) for i in range(rows)])

        def up(a, first, last):
            return lax.ppermute(a, "slopes", [(i * ny + j, (i + 1) * ny + j) for i in range(first, last) for j in range(ny)])

        def down(a, first, last):
            return lax.ppermute(a, "slopes", [(i * ny + j, (i - 1) * ny + j) for i in range(first, last) for j in range(ny)])

        def gather_z(a):
            got = [(a, z)]
            above, below = a, a
            for t in range(1, nz):
                above = down(above, 1, nz - t + 1)
                below = up(below, t - 1, nz - 1)
                got.append((above, z + t))
                got.append((below, z - t))
            return got

        def place(blocks, n):
            first = blocks[0][0]
            out = jnp.zeros((n, *first.shape), first.dtype)
            for block, at in blocks:
                ok = (at >= 0) & (at < n)
                spot = jnp.clip(at, 0, n - 1)
                old = lax.dynamic_index_in_dim(out, spot, 0, keepdims=False)
                out = lax.dynamic_update_index_in_dim(out, jnp.where(ok, block, old), spot, 0)
            return out

        def scatter_z(part, send):
            from_below = from_above = None
            for t in range(1, nz):
                qa, qb = z + nz - t, z - nz + t
                both = 2 * t - 1 >= nz
                if both:
                    ups = part(jnp.clip(qa, 0, nz - 1))
                    downs = part(jnp.clip(qb, 0, nz - 1))
                    if from_below is not None:
                        ups, downs = ups + from_below, downs + from_above
                else:
                    ups = part(jnp.where(z <= t - 1, jnp.clip(qa, 0, nz - 1), jnp.clip(qb, 0, nz - 1)))
                    if from_below is not None:
                        ups = ups + from_below + from_above
                    downs = ups
                from_below = up(ups.astype(send), 0, min(t, nz - 1)).astype(F32)
                from_above = down(downs.astype(send), max(nz - t, 1), nz).astype(F32)
            return part(z) + from_below + from_above

        def halves(a, axis):
            n = a.shape[axis] // ny
            return lax.dynamic_slice_in_dim(a, y * n, n, axis), lax.dynamic_slice_in_dim(a, (1 - y) * n, n, axis)

        def joined(own, other, axis):
            return jnp.where(y == 0, jnp.concatenate([own, other], axis), jnp.concatenate([other, own], axis))

        def gather_rows(a):
            got = [a] + [to_x(a, k) for k in range(1, nx)]
            return [v for a in got for v in (a, to_core(a))]

        def owner(i):
            k, c = i // CORES, i % CORES
            return ((x - k) % nx) * CORES + ((r % CORES) ^ c)

        def spot(q):
            return ((x - q // CORES) % nx) * CORES + ((r % CORES) ^ (q % CORES))

        keep, give = halves(propagation, 0)
        got1 = to_y(give)
        low = residual_in.astype(BF)
        rkeep, rgive = halves(low, 0)
        rline = jnp.concatenate([rkeep, to_y(rgive)], 1)
        line = jnp.concatenate([keep, got1], 1)
        got2 = to_y(keep)
        blocks = [jnp.concatenate([line, jnp.concatenate([give, got2], 1)], 0)]
        for k in range(1, nx):
            xkeep, xgive, xgot1 = to_x(keep, k), to_x(give, k), to_x(got1, k)
            xgot2 = to_y(xkeep)
            blocks.append(jnp.concatenate([jnp.concatenate([xkeep, xgot1], 1), jnp.concatenate([xgive, xgot2], 1)], 0))
        dall = jnp.stack([v for b in blocks for v in (b, to_core(b))])
        dlines = place(gather_z(line), nz)

        cov_t = cov_slab.T
        covs = place([(b, owner(i)) for i, b in enumerate(gather_rows(cov_t))], rows)
        covs = covs.reshape(slab, cov_t.shape[1])
        partial = dot(reconstructor, covs, 1, 1)
        pkeep, pgive = halves(partial, 0)
        pkeep = pkeep + to_y(pgive)
        piece = h // nz
        ureach = scatter_z(lambda q: lax.dynamic_slice_in_dim(pkeep, q * piece, piece, 0), F32)
        ukeep = place(gather_z(ureach.astype(BF)), nz).reshape(h, slab)
        uother = to_y(ukeep)
        urel = jnp.concatenate([ukeep, uother], 0)

        vt = reconstructor[:, ::stride].T
        vt = joined(vt, to_y(vt), 0)
        vt = place(gather_z(vt), nz).reshape(slab, m)
        vt = jnp.concatenate(halves(vt, 1), 1)
        vts = gather_rows(vt)
        vmine = lax.dynamic_index_in_dim(jnp.stack([v[:, :h] for v in vts]), spot(z), 0, keepdims=False)
        residual_out = residual_in + dot(joined(ukeep, uother, 0), vmine, 1, 0)

        def part(q):
            return dot(rline, lax.dynamic_index_in_dim(dall, spot(q), 0, keepdims=False), 1, 1)

        yown = scatter_z(part, BF).astype(BF)
        yturn = jnp.concatenate([yown[:, h:], yown[:, :h]], 1)
        yy = to_y(yturn)
        mine = jnp.concatenate([yown, yy], 0)
        ys = gather_rows(mine)
        dparts = [lax.dynamic_index_in_dim(dlines, owner(i), 0, keepdims=False) for i in range(rows)]
        front = sum(dot(a, b, 1, 0) for a, b in zip(dparts, ys))
        other = to_y(front[:, h:])

        du = sum(dot(a, b, 1, 0) for a, b in zip(dparts, gather_rows(urel))).astype(BF)
        dv = sum(dot(a, b, 1, 1) for a, b in zip(dparts, vts)).astype(BF)
        dvs = gather_rows(dv)
        dvmine = lax.dynamic_index_in_dim(jnp.stack(dvs), spot(z), 0, keepdims=False)
        projected = joined(front[:, :h], other, 0) + dot(joined(du, to_y(du), 0), dvmine, 1, 1)
        return residual_out, projected

    return body


def solution(mesh):
    placed = (P("rows", "slopes"), P("slopes", "rows"), P("rows", "slopes"), P("rows", "slopes"))
    return jax.shard_map(
        make_body(mesh.shape["rows"], mesh.shape["slopes"]),
        mesh=mesh,
        in_specs=placed,
        out_specs=(P("rows", "slopes"), P("rows", "slopes")),
        check_vma=False,
    )
```
